512 devices in a mesh: sa: 16 (over z_lo, core), sb: 16 (over y, x), noise: 2 (over z_hi).
Axes of the slice: x: 4, y: 4, z: 16 (z_hi: 2, z_lo: 8; z = z_hi * 8 + z_lo), core: 2. Of those that a mesh axis runs over, the one named last changes fastest.
Arguments:
- base: bfloat16 [8192, 1536], P(('sa', 'sb')), may hold values from -6 to 6
- noise: bfloat16 [4, 8192, 1536], P('noise', ('sa', 'sb')), may hold values from -3 to 3
- cot: bfloat16 [8192, 1536], P(('sa', 'sb')), may hold values from -6 to 6
- convolution_weight: bfloat16 [3, 1536, 384], P(None, 'sa'), may hold values from -0.15625 to 0.15625
- mix_w: bfloat16 [384, 1536], P('sa'), may hold values from -0.625 to 0.625
- norm_gain: float32 [1536], replicated, may hold values from 0.1 to 1.9
- qkv_w: bfloat16 [1536, 896], P('sa'), may hold values from -1 to 1
- out_w: bfloat16 [384, 1536], P('sa'), may hold values from -1.25 to 1.25
- band_width: int32 [4], replicated, may hold values from 1 to 32, as said below
- pairs: int32 [64, 2], replicated, may hold values from 0 to 63, as said below
Outputs:
- saliency: float32 [8192, 1536], P(('sa', 'sb'))
The draws below stay inside these ranges and needn't reach their ends.
Inputs may be any that keep to these rules, and one draw needn't show every extreme that they name: `band_width`: one head has band half-width exactly 32. Tile t holds bins t * 128 to (t + 1) * 128 - 1; both tiles of a pair lie in the same stretch of 512 bins that starts at a multiple of 512; pairs may repeat.
All inputs are finite; a program needn't handle non-finite values.
Results may differ from the reference program's by a relative error of at most 0.018.
Values may be sent and summed in bfloat16 or wider, within the bound.
A program may use at most 64 MiB of HBM per device.

```python
import jax
import jax.numpy as jnp
from jax import lax

D = 1536
HID = 384
HEADS = 4
KEY = 64
VAL = 96
DILATION_BINS = 16
BAND = 32
TILE = 128
PAIRS_STR = 4
BINS_DEV = 32
QKV = 896
STRETCH = 512
LENGTH = 8192
SAMPLES = 4
TILES = 64
NPAIRS = 64
N_SA = 16
N_SB = 16


def draw_qkv_w(key, part):
    values = jax.random.normal(key, (D, QKV), jnp.float32) * D ** (-0.5)
    return jnp.clip(values, -1.0, 1.0).astype(jnp.bfloat16)


def draw_band_width(key, part):
    first, second = jax.random.split(jax.random.fold_in(key, 17))
    widths = jax.random.randint(first, (HEADS,), 1, BAND + 1, dtype=jnp.int32)
    chosen = jax.random.randint(second, (), 0, HEADS, dtype=jnp.int32)
    return jnp.where(jnp.arange(HEADS, dtype=jnp.int32) == chosen, BAND, widths).astype(jnp.int32)


def draw_pairs(key, part):
    per_stretch = STRETCH // TILE
    subkeys = jax.random.split(key, 3)
    stretch_id = jnp.repeat(jnp.arange(N_SA, dtype=jnp.int32), PAIRS_STR)
    first_pick = jax.random.randint(subkeys[0], (NPAIRS,), 0, per_stretch, dtype=jnp.int32)
    second_pick = jax.random.randint(subkeys[1], (NPAIRS,), 0, per_stretch, dtype=jnp.int32)
    query_tile = stretch_id * per_stretch + first_pick * second_pick // per_stretch
    key_tile = stretch_id * per_stretch + jax.random.randint(subkeys[2], (NPAIRS,), 0, per_stretch, dtype=jnp.int32)
    return jnp.stack([query_tile, key_tile], axis=1).astype(jnp.int32)


def level_of(own_key, dims, cuts, least, largest):
    loudness = 1.0
    for position, shards_of in cuts:
        steps = jax.random.uniform(jax.random.fold_in(jax.random.fold_in(own_key, 6), position), (shards_of,), jnp.float32, least / len(cuts), largest / len(cuts))
        loudness = loudness * jnp.repeat(jnp.exp(steps), dims[position] // shards_of).reshape((-1,) + (1,) * (len(dims) - 1 - position))
    return loudness


def scatter_about(own_key, extent, spread, most, cuts=(), kind=jnp.bfloat16):
    loudness = level_of(own_key, extent, cuts, -0.22, 0.18) if cuts else 1.0
    array = jax.random.normal(own_key, extent, jnp.float32) * spread * loudness
    return jnp.minimum(jnp.maximum(array, -most), most).astype(kind)


def setup_inputs(seed: int = 0) -> dict:
    keys = jax.random.split(jax.random.key(seed), 11)
    base = scatter_about(keys[0], (LENGTH, D), 1.0, 6.0, ((0, 256),))
    noise = scatter_about(keys[1], (SAMPLES, LENGTH, D), 0.5, 3.0, ((0, 2), (1, 256)))
    cot = scatter_about(keys[2], (LENGTH, D), 1.0, 6.0, ((0, 256),))
    convolution_weight = scatter_about(keys[3], (3, D, HID), D ** -0.5, 0.15625, ((1, 16),))
    mix_w = scatter_about(keys[4], (HID, D), (HID // 4) ** -0.5, 0.625, ((0, 16),))
    norm_gain = jnp.clip(1.0 + 0.18 * jax.random.normal(keys[5], (D,), jnp.float32), 0.1, 1.9)
    qkv_w = draw_qkv_w(jax.random.fold_in(keys[10], 71), 0)
    out_w = scatter_about(keys[7], (HEADS * VAL, D), (HEADS * VAL // 16) ** -0.5, 1.25, ((0, 16),))
    band_width = draw_band_width(jax.random.fold_in(keys[10], 71), 0)
    pairs = draw_pairs(jax.random.fold_in(keys[10], 71), 0)
    return {"base": base, "noise": noise, "cot": cot, "convolution_weight": convolution_weight, "mix_w": mix_w, "norm_gain": norm_gain, "qkv_w": qkv_w, "out_w": out_w, "band_width": band_width, "pairs": pairs}


ROOT_TWO_PI = 0.7978845608
CUBIC = 0.044715

def gelu_tanh(values):
    inner = ROOT_TWO_PI * (values + CUBIC * values * values * values)
    return 0.5 * values * (1.0 + jnp.tanh(inner))

def gelu_slope(values):
    tangent = jnp.tanh(ROOT_TWO_PI * (values + CUBIC * values * values * values))
    return 0.5 * (1.0 + tangent) + 0.5 * values * (1.0 - tangent * tangent) * ROOT_TWO_PI * (1.0 + 3.0 * CUBIC * values * values)

def rounded(values):
    return lax.optimization_barrier(values.astype(jnp.bfloat16)).astype(jnp.float32)

def reference(base, noise, cot, convolution_weight, mix_w, norm_gain, qkv_w, out_w, band_width, pairs):
    sequence_length = base.shape[0]
    heads_key = HEADS * KEY
    heads_val = HEADS * VAL
    scale = KEY ** (-0.5)
    tile_ids = jnp.arange(TILES, dtype=jnp.int32)
    pick_query = (pairs[:, 0][:, None] == tile_ids[None, :]).astype(jnp.float32)
    pick_key = (pairs[:, 1][:, None] == tile_ids[None, :]).astype(jnp.float32)
    table = jnp.dot(pick_query.T, pick_key) > 0.5
    d_att = jnp.dot(cot, out_w.T, preferred_element_type=jnp.float32).astype(jnp.bfloat16)
    d_att_heads = d_att.reshape(sequence_length, HEADS, VAL)
    width = STRETCH + 2 * BAND
    blocks = sequence_length // BINS_DEV

    def one_sample(noise_row):
        noisy = base.astype(jnp.float32) + noise_row.astype(jnp.float32)
        gelu_input = gelu_tanh(noisy).astype(jnp.bfloat16)
        padded_input = jnp.pad(gelu_input, ((DILATION_BINS, DILATION_BINS), (0, 0)))
        hidden_state = jnp.zeros((sequence_length, HID), jnp.float32)
        for tap_index in range(3):
            hidden_state = hidden_state + jnp.dot(padded_input[tap_index * DILATION_BINS:tap_index * DILATION_BINS + sequence_length], convolution_weight[tap_index], preferred_element_type=jnp.float32)
        act = gelu_tanh(hidden_state).astype(jnp.bfloat16)
        resid = noisy + jnp.dot(act, mix_w, preferred_element_type=jnp.float32)
        inv_rms = lax.rsqrt(lax.optimization_barrier(jnp.mean(resid * resid, axis=-1, keepdims=True)) + 1e-06)
        normed = (resid * inv_rms * norm_gain).astype(jnp.bfloat16)
        proj = jnp.dot(normed, qkv_w, preferred_element_type=jnp.float32).astype(jnp.bfloat16)
        queries = proj[:, :heads_key].reshape(sequence_length, HEADS, KEY)
        key_vals = jnp.pad(proj[:, heads_key:], ((BAND, BAND), (0, 0)))

        def step(carry, block):
            row_first = block * BINS_DEV
            stretch_id = block // N_SB
            col_first = stretch_id * STRETCH
            query_blk = lax.dynamic_slice(queries, (row_first, jnp.int32(0), jnp.int32(0)), (BINS_DEV, HEADS, KEY)).astype(jnp.float32)
            window = lax.dynamic_slice(key_vals, (col_first, jnp.int32(0)), (width, heads_key + heads_val))
            key_blk = window[:, :heads_key].reshape(width, HEADS, KEY).astype(jnp.float32)
            val_blk = window[:, heads_key:].reshape(width, HEADS, VAL).astype(jnp.float32)
            rows = row_first + jnp.arange(BINS_DEV, dtype=jnp.int32)
            cols = col_first - BAND + jnp.arange(width, dtype=jnp.int32)
            inside = (cols >= 0) & (cols < sequence_length)
            apart = jnp.abs(rows[:, None] - cols[None, :])
            in_band = apart[None] <= band_width[:, None, None]
            same = (cols >= col_first) & (cols < col_first + STRETCH)
            query_tile = rows // TILE
            key_tile = jnp.clip(cols, 0, sequence_length - 1) // TILE
            paired = table[query_tile][:, key_tile] & same[None, :]
            allowed = inside[None, None, :] & (in_band | paired[None])
            score = jnp.einsum('ihd,jhd->hij', query_blk, key_blk) * scale
            score = jnp.where(allowed, score, -1e+30)
            top = lax.optimization_barrier(jnp.max(score, axis=-1))
            total = lax.optimization_barrier(jnp.sum(jnp.where(allowed, jnp.exp(score - top[..., None]), 0.0), axis=-1))
            lse = top + jnp.log(total)
            prob = jnp.where(allowed, jnp.exp(score - lse[..., None]), 0.0)
            prob_b = rounded(prob)
            attn = jnp.einsum('hij,jhe->ihe', prob_b, val_blk)
            grad_blk = lax.dynamic_slice(d_att_heads, (row_first, jnp.int32(0), jnp.int32(0)), (BINS_DEV, HEADS, VAL)).astype(jnp.float32)
            delta = lax.optimization_barrier(jnp.sum(grad_blk * attn, axis=-1))
            d_prob = jnp.einsum('ihe,jhe->hij', grad_blk, val_blk)
            d_score = rounded(prob * (d_prob - delta.T[..., None]) * scale)
            d_query = jnp.einsum('hij,jhd->ihd', d_score, key_blk)
            d_key = jnp.einsum('hij,ihd->jhd', d_score, query_blk)
            d_value = jnp.einsum('hij,ihe->jhe', prob_b, grad_blk)
            d_window = jnp.concatenate([d_key.reshape(width, heads_key), d_value.reshape(width, heads_val)], axis=1)
            current = lax.dynamic_slice(carry, (col_first, jnp.int32(0)), (width, heads_key + heads_val))
            carry = lax.dynamic_update_slice(carry, current + d_window, (col_first, jnp.int32(0)))
            return (carry, d_query.reshape(BINS_DEV, heads_key))
        start = jnp.zeros((sequence_length + 2 * BAND, heads_key + heads_val), jnp.float32)
        d_kv_pad, d_query = lax.scan(step, start, jnp.arange(blocks, dtype=jnp.int32))
        d_query = d_query.reshape(sequence_length, heads_key)
        d_proj = jnp.concatenate([d_query, d_kv_pad[BAND:BAND + sequence_length]], axis=1).astype(jnp.bfloat16)
        d_normed = jnp.dot(d_proj, qkv_w.T, preferred_element_type=jnp.float32)
        gained = norm_gain * d_normed
        d_resid = cot.astype(jnp.float32) + inv_rms * gained - resid * inv_rms * inv_rms * inv_rms * lax.optimization_barrier(jnp.mean(resid * gained, axis=-1, keepdims=True))
        d_act = jnp.dot(d_resid.astype(jnp.bfloat16), mix_w.T, preferred_element_type=jnp.float32)
        hidden_gradient = (d_act * gelu_slope(hidden_state)).astype(jnp.bfloat16)
        gradient_padded = jnp.pad(hidden_gradient, ((DILATION_BINS, DILATION_BINS), (0, 0)))
        d_gelu_in = jnp.zeros((sequence_length, D), jnp.float32)
        for tap_index in range(3):
            start_offset = (2 - tap_index) * DILATION_BINS
            d_gelu_in = d_gelu_in + jnp.dot(gradient_padded[start_offset:start_offset + sequence_length], convolution_weight[tap_index].T, preferred_element_type=jnp.float32)
        return d_resid + d_gelu_in * gelu_slope(noisy)
    summed = jnp.zeros((sequence_length, D), jnp.float32)
    for sample in range(SAMPLES):
        summed = summed + one_sample(noise[sample])
    return summed / SAMPLES
```

```python
import functools

import jax
import jax.numpy as jnp
from jax import lax
from jax.experimental import pallas as pl
from jax.experimental.pallas import tpu as pltpu
from jax.sharding import PartitionSpec as P

MESH = pl.DeviceIdType.MESH
D = 1536
HID = 384
HEADS = 4
KEY = 64
VAL = 96
HK = HEADS * KEY
HV = HEADS * VAL
QKV = 2 * HK + HV
DIL = 16
BAND = 32
TILE = 128
BINS = 32
NS = 2
ROWS = NS * BINS
STRETCH = 512
LENGTH = 8192
CELLS = 640
SA = 16
LAST = 15
ROOT_TWO_PI = 0.7978845608
CUBIC = 0.044715
F32 = jnp.float32
BF16 = jnp.bfloat16
Z_STEPS = (1, -1, 2, -2, 3, -3, 4)
NSEM = 200


def gelu_and_slope(v):
    tangent = jnp.tanh(ROOT_TWO_PI * (v + CUBIC * v * v * v))
    half = 0.5 * (1.0 + tangent)
    slope = half + 0.5 * v * (1.0 - tangent * tangent) * ROOT_TWO_PI * (1.0 + 3.0 * CUBIC * v * v)
    return v * half, slope


def dot(a, b):
    return lax.dot_general(a, b, (((1,), (0,)), ((), ())), preferred_element_type=F32)


def dot_t(a, b):
    return lax.dot_general(a, b, (((1,), (1,)), ((), ())), preferred_element_type=F32)


def dot_l(a, b):
    return lax.dot_general(a, b, (((0,), (0,)), ((), ())), preferred_element_type=F32)


def lane_heads(value, width):
    lanes = lax.broadcasted_iota(jnp.int32, value.shape, 1)
    return [jnp.where((lanes >= h * width) & (lanes < (h + 1) * width), value, jnp.zeros_like(value)) for h in range(HEADS)]


def stack_heads(value, width):
    return jnp.concatenate(lane_heads(value, width), axis=0)


def unstack_heads(value, width):
    rows = value.shape[0] // HEADS
    lanes = lax.broadcasted_iota(jnp.int32, (rows, value.shape[1]), 1)
    total = jnp.zeros((rows, value.shape[1]), F32)
    for h in range(HEADS):
        part = value[h * rows : (h + 1) * rows]
        total = total + jnp.where((lanes >= h * width) & (lanes < (h + 1) * width), part, 0.0)
    return total


def kernel(
    base_ref, noise_ref, cot_ref, conv_ref, mix_ref, gain_ref, qkv_ref, outw_ref, bw_ref, pairs_ref,
    out_ref,
    base_v, noise_v, cot_v, noisy_v, slope_v, gext, conv_v, mix_v, qkv_v, outw_v,
    resid_v, proj_v, datt_v, stat_v, mask_q, mask_k, hgext, sum_v, far_v,
    ssem, rsem, lsem,
):
    sa, sb, hi = lax.axis_index("sa"), lax.axis_index("sb"), lax.axis_index("noise")
    zl, core = sa // 2, sa % 2
    y, x = sb // 4, sb % 4
    zf = hi * 8 + zl
    me = (sa, sb, hi)

    def at_z(d):
        z = (zf + d + 16) % 16
        return ((z % 8) * 2 + core, sb, z // 8)

    sibling = (zl * 2 + 1 - core, sb, hi)
    partner = (sa, sb, 1 - hi)

    def at_x(d):
        return (sa, y * 4 + (x + d + 4) % 4, hi)

    def at_y(d):
        return (sa, ((y + d + 4) % 4) * 4 + x, hi)

    cell = sa * 16 + sb
    left_cell, right_cell = cell - 1, cell + 1
    has_left, has_right = cell > 0, cell < 255
    left = ((left_cell + 256) % 256 // 16, (left_cell + 256) % 16, hi)
    right = (right_cell % 256 // 16, right_cell % 16, hi)
    edge_left = (sb == 0) & (sa > 0)
    edge_right = (sb == LAST) & (sa < SA - 1)

    count = [0]
    pending = []

    def remote(src, dst, device):
        n = count[0]
        count[0] += 1
        return pltpu.make_async_remote_copy(
            src_ref=src, dst_ref=dst, send_sem=ssem.at[n], recv_sem=rsem.at[n], device_id=device, device_id_type=MESH
        )

    def send(src, dst, device):
        copy = remote(src, dst, device)
        copy.start()
        pending.append(copy)
        return copy

    local = []

    def fetch(src, dst):
        copy = pltpu.make_async_copy(src, dst, lsem.at[len(local)])
        copy.start()
        local.append(copy)
        return copy

    got_base = fetch(base_ref, base_v)
    got_noise = fetch(noise_ref, noise_v)
    got_cot = fetch(cot_ref, cot_v)

    def cols(p):
        return pl.ds(pl.multiple_of(p * 384, 128), 384)

    def rows(p):
        return pl.ds(pl.multiple_of(p * 24, 8), 24)

    def conv_item(tap, first, width):
        c = pl.ds(first, width)
        return (
            lambda p: conv_ref.at[tap, rows(p), c],
            lambda z, k, p: conv_v.at[tap, z, k, p, :, c],
        )

    def qkv_item(first, width):
        c = pl.ds(first, width)
        return (lambda p: qkv_ref.at[rows(p), c], lambda z, k, p: qkv_v.at[z, k, p, :, c])

    def col_item(source, gathered):
        return (lambda p: source.at[:, cols(p)], lambda z, k, p: gathered.at[z, k, :, cols(p)])

    def col_all(gathered):
        return lambda k: gathered.at[:, k]

    every = pl.ds(0, 8)
    low, high = pl.ds(0, 4), pl.ds(4, 4)
    items = [
        (conv_item(0, 0, 384), "x", lambda k: conv_v.at[0, :, k]),
        (conv_item(2, 0, 384), "y", lambda k: conv_v.at[2, :, k]),
        (conv_item(1, 0, 256), "x", lambda k: conv_v.at[1, :, k, :, :, pl.ds(0, 256)]),
        (conv_item(1, 256, 128), "y", lambda k: conv_v.at[1, :, k, :, :, pl.ds(256, 128)]),
        (col_item(mix_ref, mix_v), "y", col_all(mix_v)),
        (qkv_item(512, 384), "x", lambda k: qkv_v.at[:, k, :, :, pl.ds(512, 384)]),
        (qkv_item(0, 512), "y", lambda k: qkv_v.at[:, k, :, :, pl.ds(0, 512)]),
        (col_item(outw_ref, outw_v), "x", col_all(outw_v)),
    ]
    own_piece = []
    for (source, slot), route, _ in items:
        p = x if route == "x" else y
        own_piece.append(fetch(source(p), slot(zl, core, p)))

    barrier = pltpu.get_barrier_semaphore()
    peers = [at_z(d) for d in (1, -1, 2, -2, 3, -3, 4, -4)] + [sibling, partner]
    for dy in range(4):
        for dx in range(4):
            if dy or dx:
                peers.append((sa, ((y + dy) % 4) * 4 + (x + dx) % 4, hi))
    for device in peers:
        pl.semaphore_signal(barrier, inc=1, device_id=device, device_id_type=MESH)

    @pl.when(edge_left)
    def _():
        pl.semaphore_signal(barrier, inc=1, device_id=left, device_id_type=MESH)

    @pl.when(edge_right)
    def _():
        pl.semaphore_signal(barrier, inc=1, device_id=right, device_id_type=MESH)

    pl.semaphore_wait(barrier, len(peers) + jnp.where(edge_left | edge_right, 1, 0).astype(jnp.int32))

    z_copies = []
    for (source, slot), route, _ in items:
        p = x if route == "x" else y
        z_copies.append([send(source(p), slot(zl, core, p), at_z(d)) for d in Z_STEPS])

    got_base.wait()
    got_noise.wait()
    for n in range(NS):
        noisy = base_v[...].astype(F32) + noise_v[n].astype(F32)
        noisy_v[pl.ds(n * BINS, BINS), :] = noisy
        gelu, slope = gelu_and_slope(noisy)
        gext[n, pl.ds(DIL, BINS), :] = gelu.astype(BF16)
        slope_v[pl.ds(n * BINS, BINS), :] = slope

    def edge_copy(src, dst, device, condition):
        copy = remote(src, dst, device)

        @pl.when(condition)
        def _():
            copy.start()

        return copy

    def edge_wait(copy, sent, received):
        @pl.when(received)
        def _():
            copy.wait_recv()

        @pl.when(sent)
        def _():
            copy.wait_send()

    halo_l = edge_copy(gext.at[:, pl.ds(DIL, DIL), :], gext.at[:, pl.ds(DIL + BINS, DIL), :], left, has_left)
    halo_r = edge_copy(gext.at[:, pl.ds(BINS, DIL), :], gext.at[:, pl.ds(0, DIL), :], right, has_right)

    @pl.when(jnp.logical_not(has_left))
    def _():
        gext[:, pl.ds(0, DIL), :] = jnp.zeros((NS, DIL, D), BF16)
        hgext[:, pl.ds(0, DIL), :] = jnp.zeros((NS, DIL, HID), BF16)

    @pl.when(jnp.logical_not(has_right))
    def _():
        gext[:, pl.ds(DIL + BINS, DIL), :] = jnp.zeros((NS, DIL, D), BF16)
        hgext[:, pl.ds(DIL + BINS, DIL), :] = jnp.zeros((NS, DIL, HID), BF16)

    def clear(slot):
        proj_v[:, 4, slot] = jnp.zeros((NS, BINS, QKV), BF16)
        datt_v[4, slot] = jnp.zeros((BINS, HV), BF16)
        stat_v[4, slot] = jnp.zeros((8, 128), F32)

    clear(2)
    clear(3)

    @pl.when(jnp.logical_not(edge_left))
    def _():
        clear(0)

    @pl.when(jnp.logical_not(edge_right))
    def _():
        clear(1)

    first_row = cell * BINS
    first_col = sa * STRETCH
    tile_own = sa * 4 + sb // 4
    p0, p1 = pairs_ref[:, 0:1], pairs_ref[:, 1:2]

    def flag(a, b):
        return jnp.max(jnp.where((p0 == a) & (p1 == b), 1.0, 0.0), axis=0, keepdims=True)

    def band_of(index):
        wide = jnp.full(index.shape, bw_ref[0], jnp.int32)
        for h in range(1, HEADS):
            wide = jnp.where(index // BINS == h, bw_ref[h], wide)
        return wide

    def mask_of(shape, cells_dim, flags):
        r = lax.broadcasted_iota(jnp.int32, shape, cells_dim)
        hi_ = lax.broadcasted_iota(jnp.int32, shape, 1 - cells_dim)
        away = jnp.where(r < 512, r, jnp.where(r < 544, r - 544, r - 32))
        pos = first_col + away
        valid = (r < 576) & (pos >= 0) & (pos < LENGTH)
        own = first_row + hi_ % BINS
        in_band = jnp.abs(pos - own) <= band_of(hi_)
        paired = jnp.zeros(shape, F32)
        for t in range(4):
            paired = jnp.where((r >= t * TILE) & (r < (t + 1) * TILE), jnp.broadcast_to(flags[t], shape), paired)
        return jnp.where(valid & (in_band | (paired > 0.5)), 1.0, 0.0)

    mask_q[...] = mask_of((CELLS, 128), 0, [flag(tile_own, sa * 4 + t) for t in range(4)])
    mask_k[...] = mask_of((128, CELLS), 1, [flag(sa * 4 + t, tile_own) for t in range(4)])

    def ring(view, halves, index, device):
        right_copy = send(view(index), view(index), device(1))
        left_copy = send(view(index), view(index), device(-1))

        def forward():
            right_copy.wait_recv()
            a = send(halves((index + 3) % 4, 0), halves((index + 3) % 4, 0), device(1))
            left_copy.wait_recv()
            b = send(halves((index + 1) % 4, 1), halves((index + 1) % 4, 1), device(-1))

            def finish():
                a.wait_recv()
                b.wait_recv()

            return finish

        return forward

    swaps = [None] * len(items)
    forwards = [None] * len(items)
    finishes = [None] * len(items)

    def stage_a(i):
        (source, slot), route, _ = items[i]
        own_piece[i].wait()
        for copy in z_copies[i]:
            copy.wait_recv()
        forwards[i] = ring(
            lambda p: slot(every, core, p),
            lambda p, half: slot(low if half == 0 else high, core, p),
            x if route == "x" else y,
            at_x if route == "x" else at_y,
        )

    def stage_b(i):
        finishes[i] = forwards[i]()

    def stage_c(i):
        finishes[i]()
        whole = items[i][2]
        swaps[i] = send(whole(core), whole(core), sibling)

    stage_a(0)
    stage_a(1)
    stage_a(2)
    stage_a(3)
    stage_b(0)
    stage_b(1)
    stage_a(4)
    stage_b(2)
    stage_b(3)
    stage_c(0)
    stage_c(1)
    stage_a(5)
    stage_a(6)
    stage_b(4)
    stage_c(2)
    stage_c(3)
    stage_a(7)
    stage_b(5)
    stage_b(6)
    stage_c(4)

    edge_wait(halo_r, has_right, has_left)
    edge_wait(halo_l, has_left, has_right)

    def tap_of(ref, t):
        return ref[:, pl.ds(t * DIL, BINS), :].reshape(ROWS, ref.shape[2])

    swaps[0].wait_recv()
    hidden = dot(tap_of(gext, 0), conv_v[0].reshape(D, HID))
    stage_b(7)
    swaps[1].wait_recv()
    hidden = hidden + dot(tap_of(gext, 2), conv_v[2].reshape(D, HID))
    stage_c(5)
    stage_c(6)
    swaps[2].wait_recv()
    swaps[3].wait_recv()
    hidden = hidden + dot(tap_of(gext, 1), conv_v[1].reshape(D, HID))
    act, hidden_slope = gelu_and_slope(hidden)
    stage_c(7)
    swaps[4].wait_recv()
    resid = noisy_v[...] + dot(act.astype(BF16), mix_v[...].reshape(HID, D))
    resid_v[...] = resid
    inv_rms = lax.rsqrt(jnp.mean(resid * resid, axis=1, keepdims=True) + 1e-06)
    gain = gain_ref[...]
    normed = (resid * inv_rms * gain).astype(BF16)
    swaps[5].wait_recv()
    swaps[6].wait_recv()
    proj = dot(normed, qkv_v[...].reshape(D, QKV)).astype(BF16)
    for n in range(NS):
        proj_v[n, y, x] = proj[n * BINS : (n + 1) * BINS]

    def gather(ref_of, split):
        def first(n):
            def view(i):
                return ref_of(n, y, i, None) if n == 0 else ref_of(n, i, x, None)

            def halves(i, half):
                return ref_of(n, y, i, half) if n == 0 else ref_of(n, i, x, half)

            return ring(view, halves, x if n == 0 else y, at_x if n == 0 else at_y)

        def second(n):
            def view(i):
                return ref_of(n, i, pl.ds(0, 4), None) if n == 0 else ref_of(n, pl.ds(0, 4), i, None)

            def halves(i, half):
                part = pl.ds(2 * half, 2)
                return ref_of(n, i, part, None) if n == 0 else ref_of(n, part, i, None)

            return ring(view, halves, y if n == 0 else x, at_y if n == 0 else at_x)

        return first, second

    def span(rows_, half):
        return pl.ds(0, rows_) if half is None else pl.ds(half * (rows_ // 2), rows_ // 2)

    def kv_ref(n, i, j, half):
        return proj_v.at[n, i, j, span(BINS, half), pl.ds(HK, HK + HV)]

    def q_ref(n, i, j, half):
        return proj_v.at[n, i, j, span(BINS, half), pl.ds(0, HK)]

    def d_ref(n, i, j, half):
        quarter = pl.ds(n * 16, 16) if half is None else pl.ds(n * 16 + half * 8, 8)
        return datt_v.at[i, j, quarter, :]

    kv_first, kv_second = gather(kv_ref, None)
    q_first, q_second = gather(q_ref, None)
    d_first, d_second = gather(d_ref, None)

    kv_f = [kv_first(0), kv_first(1)]
    ext_l = edge_copy(proj_v.at[:, y, x], proj_v.at[:, 4, 1], left, edge_left)
    ext_r = edge_copy(proj_v.at[:, y, x], proj_v.at[:, 4, 0], right, edge_right)
    kv_g = [f() for f in kv_f]

    got_cot.wait()
    swaps[7].wait_recv()
    d_att = dot_t(cot_v[...], outw_v[...].reshape(HV, D)).astype(BF16)
    datt_v[y, x] = d_att
    dext_l = edge_copy(datt_v.at[y, x], datt_v.at[4, 1], left, edge_left)
    dext_r = edge_copy(datt_v.at[y, x], datt_v.at[4, 0], right, edge_right)

    for g in kv_g:
        g()
    kv_f = [kv_second(0), kv_second(1)]
    q_f = [q_first(0), q_first(1)]
    d_f = [d_first(0), d_first(1)]
    d_stack = stack_heads(d_att, VAL)
    kv_g = [f() for f in kv_f]
    q_g = [f() for f in q_f]
    d_g = [f() for f in d_f]
    edge_wait(ext_r, edge_right, edge_left)
    edge_wait(ext_l, edge_left, edge_right)
    for g in kv_g:
        g()
    for g in q_g + d_g:
        g()
    q_f = [q_second(0), q_second(1)]
    d_f = [d_second(0), d_second(1)]

    allowed = mask_q[...] > 0.5
    scale = KEY ** (-0.5)
    d_query = []
    stats = []
    for n in range(NS):
        k_all = proj_v[n, :, :, :, pl.ds(HK, HK)].reshape(CELLS, HK)
        v_all = proj_v[n, :, :, :, pl.ds(2 * HK, HV)].reshape(CELLS, HV)
        q_stack = stack_heads(proj[n * BINS : (n + 1) * BINS, :HK], KEY)
        score = jnp.where(allowed, dot_t(k_all, q_stack) * scale, -1e30)
        top = jnp.max(score, axis=0, keepdims=True)
        e = jnp.where(allowed, jnp.exp(score - top), 0.0)
        total = jnp.sum(e, axis=0, keepdims=True)
        prob = e / total
        d_prob = dot_t(v_all, d_stack)
        delta = jnp.sum(prob.astype(BF16).astype(F32) * d_prob, axis=0, keepdims=True)
        d_score = (prob * (d_prob - delta) * scale).astype(BF16)
        d_query.append(unstack_heads(dot_l(d_score, k_all), KEY))
        stats.append((top + jnp.log(total), delta))
    line = lax.broadcasted_iota(jnp.int32, (8, 128), 0)
    table = jnp.zeros((8, 128), F32)
    for n in range(NS):
        table = jnp.where(line == n, jnp.broadcast_to(stats[n][0], (8, 128)), table)
        table = jnp.where(line == 2 + n, jnp.broadcast_to(stats[n][1], (8, 128)), table)
    stat_v[y, x] = table
    stat_copies = []
    for dy in range(4):
        for dx in range(4):
            if dy or dx:
                stat_copies.append(
                    send(stat_v.at[y, x], stat_v.at[y, x], (sa, ((y + dy) % 4) * 4 + (x + dx) % 4, hi))
                )
    sext_l = edge_copy(stat_v.at[y, x], stat_v.at[4, 1], left, edge_left)
    sext_r = edge_copy(stat_v.at[y, x], stat_v.at[4, 0], right, edge_right)

    q_g = [f() for f in q_f]
    d_g = [f() for f in d_f]
    edge_wait(dext_r, edge_right, edge_left)
    edge_wait(dext_l, edge_left, edge_right)
    for g in q_g + d_g:
        g()

    allowed_k = mask_k[...] > 0.5
    d_all = datt_v[...].reshape(CELLS, HV)
    score_k, d_prob_k, q_alls = [], [], []
    for n in range(NS):
        q_all = proj_v[n, :, :, :, pl.ds(0, HK)].reshape(CELLS, HK)
        own = proj[n * BINS : (n + 1) * BINS]
        score_k.append(dot_t(stack_heads(own[:, HK : 2 * HK], KEY), q_all) * scale)
        d_prob_k.append(dot_t(stack_heads(own[:, 2 * HK :], VAL), d_all))
        q_alls.append(q_all)
    for copy in stat_copies:
        copy.wait_recv()
    edge_wait(sext_r, edge_right, edge_left)
    edge_wait(sext_l, edge_left, edge_right)
    cells = stat_v[...]
    lanes = lax.broadcasted_iota(jnp.int32, (8, 128), 1)
    by_head = []
    for h in range(HEADS):
        groups = []
        for g in range(5):
            part = jnp.zeros((8, 128), F32)
            for k in range(4):
                only = jnp.where(lanes // BINS == h, cells[g, k], 0.0)
                shift = (BINS * (k - h)) % 128
                part = part + (pltpu.roll(only, shift, 1) if shift else only)
            groups.append(part)
        by_head.append(jnp.concatenate(groups, axis=1))

    def spread(r):
        return jnp.concatenate([jnp.broadcast_to(by_head[h][r : r + 1], (BINS, CELLS)) for h in range(HEADS)], axis=0)

    pieces = []
    for n in range(NS):
        prob_k = jnp.where(allowed_k, jnp.exp(score_k[n] - spread(n)), 0.0)
        d_val = unstack_heads(dot(prob_k.astype(BF16), d_all), VAL)
        d_sk = (prob_k * (d_prob_k[n] - spread(2 + n)) * scale).astype(BF16)
        d_key = unstack_heads(dot(d_sk, q_alls[n]), KEY)
        pieces.append(jnp.concatenate([d_query[n], d_key, d_val], axis=1).astype(BF16))
    d_proj = jnp.concatenate(pieces, axis=0)

    gained = gain * dot_t(d_proj, qkv_v[...].reshape(D, QKV))
    resid = resid_v[...]
    cot = cot_v[...].astype(F32)
    mean = jnp.mean(resid * gained, axis=1, keepdims=True)
    d_resid = (
        jnp.concatenate([cot, cot], axis=0)
        + inv_rms * gained
        - resid * (inv_rms * inv_rms * inv_rms * mean)
    )
    d_act = dot_t(d_resid.astype(BF16), mix_v[...].reshape(HID, D))
    hg = (d_act * hidden_slope).astype(BF16)
    for n in range(NS):
        hgext[n, pl.ds(DIL, BINS), :] = hg[n * BINS : (n + 1) * BINS]
    back_l = edge_copy(hgext.at[:, pl.ds(DIL, DIL), :], hgext.at[:, pl.ds(DIL + BINS, DIL), :], left, has_left)
    back_r = edge_copy(hgext.at[:, pl.ds(BINS, DIL), :], hgext.at[:, pl.ds(0, DIL), :], right, has_right)
    resid_v[...] = d_resid
    edge_wait(back_r, has_right, has_left)
    edge_wait(back_l, has_left, has_right)

    finals = []
    for chunk in range(2):
        c = pl.ds(chunk * 768, 768)
        grad_in = jnp.zeros((ROWS, 768), F32)
        for t in range(3):
            grad_in = grad_in + dot_t(tap_of(hgext, 2 - t), conv_v[t, pl.ds(chunk * 4, 4)].reshape(768, HID))
        grad = resid_v[:, c] + grad_in * slope_v[:, c]
        sum_v[:, c] = (grad[:BINS] + grad[BINS:]).astype(BF16)
        finals.append((c, send(sum_v.at[:, c], far_v.at[:, c], partner)))
    for c, copy in finals:
        copy.wait_recv()
        out_ref[:, c] = (sum_v[:, c].astype(F32) + far_v[:, c].astype(F32)) * 0.25
    for copy in pending:
        copy.wait_send()


def shards(base, noise, cot, convolution_weight, mix_w, norm_gain, qkv_w, out_w, band_width, pairs):
    anywhere = pl.BlockSpec(memory_space=pl.ANY)
    vmem = pl.BlockSpec(memory_space=pltpu.VMEM)
    smem = pl.BlockSpec(memory_space=pltpu.SMEM)
    return pl.pallas_call(
        kernel,
        out_shape=jax.ShapeDtypeStruct((BINS, D), F32),
        in_specs=[anywhere, anywhere, anywhere, anywhere, anywhere, vmem, anywhere, anywhere, smem, vmem],
        out_specs=vmem,
        scratch_shapes=[
            pltpu.VMEM((BINS, D), BF16),
            pltpu.VMEM((NS, BINS, D), BF16),
            pltpu.VMEM((BINS, D), BF16),
            pltpu.VMEM((ROWS, D), F32),
            pltpu.VMEM((ROWS, D), F32),
            pltpu.VMEM((NS, BINS + 2 * DIL, D), BF16),
            pltpu.VMEM((3, 8, 2, 4, 24, HID), BF16),
            pltpu.VMEM((8, 2, 24, D), BF16),
            pltpu.VMEM((8, 2, 4, 24, QKV), BF16),
            pltpu.VMEM((8, 2, 24, D), BF16),
            pltpu.VMEM((ROWS, D), F32),
            pltpu.VMEM((NS, 5, 4, BINS, QKV), BF16),
            pltpu.VMEM((5, 4, BINS, HV), BF16),
            pltpu.VMEM((5, 4, 8, 128), F32),
            pltpu.VMEM((CELLS, 128), F32),
            pltpu.VMEM((128, CELLS), F32),
            pltpu.VMEM((NS, BINS + 2 * DIL, HID), BF16),
            pltpu.VMEM((BINS, D), BF16),
            pltpu.VMEM((BINS, D), BF16),
            pltpu.SemaphoreType.DMA((NSEM,)),
            pltpu.SemaphoreType.DMA((NSEM,)),
            pltpu.SemaphoreType.DMA((16,)),
        ],
        compiler_params=pltpu.CompilerParams(
            collective_id=0, has_side_effects=True, vmem_limit_bytes=50 * 1024 * 1024
        ),
    )(
        base, noise, cot, convolution_weight, mix_w, norm_gain.reshape(1, D), qkv_w, out_w, band_width, pairs
    )


def solution(mesh):
    return jax.shard_map(
        shards,
        mesh=mesh,
        in_specs=(
            P(("sa", "sb"), None),
            P("noise", ("sa", "sb"), None),
            P(("sa", "sb"), None),
            P(None, "sa", None),
            P("sa", None),
            P(),
            P("sa", None),
            P("sa", None),
            P(),
            P(),
        ),
        out_specs=P(("sa", "sb"), None),
        check_vma=False,
    )
```
